32 devices in a mesh: leaf: 8 (over z, y), blk: 4 (over x, core).
Axes of the slice: x: 2, y: 2, z: 4, core: 2. Of those that a mesh axis runs over, the one named last changes fastest.
Arguments:
- leaf_net: bfloat16 [8, 64, 4096], P('leaf'), may hold values from -1.5 to 1.5
- leaf_coupling: bfloat16 [8, 4096, 4096], P('leaf', 'blk'), as said below
- index_maps: int32 [12, 32], replicated, may hold values from 0 to 35, as said below
- sep_anchor: float32 [6, 512], replicated, may hold values from 0.5 to 4
- top_net: bfloat16 [64, 32768], P(None, 'leaf'), may hold values from -1.5 to 1.5
- top_coupling: bfloat16 [32768, 2048], P('leaf', 'blk'), as said below
Outputs:
- root_update: float32 [8, 4096, 4096], P('leaf', 'blk')
- top_window: float32 [32768, 2048], P('leaf', 'blk')
The draws below stay inside these ranges and needn't reach their ends.
Inputs may be any that keep to these rules, and one draw needn't show every extreme that they name: `index_maps`: entry i of a row sends the child's block i to block entry of the parent front: values under 512 // 128 are separator blocks, value 512 // 128 + m is block m of the parent's update matrix. Each row is one-to-one and covers every separator block. A block i that goes to the update goes to a block m with m // 2 == i // 2. Each leaf_coupling[l] is symmetric, and leaf_net[l]^T leaf_net[l] + leaf_coupling[l] is positive definite. Rows 0 to 2047 of top_coupling form a symmetric matrix, and those rows of top_net^T top_net[:, :2048] + top_coupling form a positive definite matrix.
All inputs are finite; a program needn't handle non-finite values.
Results may differ from the reference program's by a relative error of at most 0.00035.
The reference program's roundings to bfloat16 on the way count: a program that leaves them out, or rounds other values in their place, can miss the bound.
Values may be sent and summed in bfloat16 or wider, within the bound.
A program may use at most 320 MiB of HBM per device.

```python
import math
import jax
import jax.numpy as jnp
from jax import lax

BS = 128
UPD = 4096
SEP = 512
RES = 16
NETS = 64
LEVELS = 2
TOP = 32768
PW = 512
NF = 2
NODES = 12
PARENTS = 6
N_LEAF = 8
N_BLK = 4


def draw_index_maps(key, part):
    upd_blocks = UPD // BS
    sep_blocks = SEP // BS
    group_size = upd_blocks // RES
    block_ids = jnp.arange(upd_blocks, dtype=jnp.int32)
    group_of = block_ids // group_size
    place_in = block_ids % group_size

    def one_node(node_num):
        node_key = jax.random.fold_in(key, node_num)
        key_groups, key_slots, key_pick = jax.random.split(node_key, 3)
        sep_groups = jax.random.permutation(key_groups, RES - 1)[:sep_blocks].astype(jnp.int32)
        slots = jax.vmap(lambda slot_key: jax.random.permutation(slot_key, group_size))(jax.random.split(key_slots, RES)).astype(jnp.int32)
        picked = jax.random.randint(key_pick, (RES,), 0, group_size).astype(jnp.int32)
        matches = sep_groups[None, :] == jnp.arange(RES, dtype=jnp.int32)[:, None]
        sep_slot = jnp.sum(jnp.where(matches, jnp.arange(sep_blocks, dtype=jnp.int32)[None, :], 0), axis=1)
        has_sep = jnp.any(matches, axis=1)
        to_update = sep_blocks + group_of * group_size + slots[group_of, place_in]
        to_sep = has_sep[group_of] & (place_in == picked[group_of])
        return jnp.where(to_sep, sep_slot[group_of], to_update).astype(jnp.int32)
    return jax.vmap(one_node)(jnp.arange(NODES, dtype=jnp.int32))


def symmetric_block(key, order):
    key_off, key_diag = jax.random.split(key, 2)
    limit_value = 1.7 / math.sqrt(order)
    raw_draw = jax.random.uniform(key_off, (order, order), jnp.float32, -limit_value, limit_value)
    cell_ids = jnp.arange(order, dtype=jnp.int32)
    off_part = jnp.where(cell_ids[:, None] < cell_ids[None, :], raw_draw, raw_draw.T)
    diagonal = jnp.exp(jax.random.uniform(key_diag, (order,), jnp.float32, math.log(4.0), math.log(16.0)))
    return jnp.where(cell_ids[:, None] == cell_ids[None, :], diagonal[:, None], off_part)


def draw_leaf_coupling(key, part):
    leaf_keys = jax.random.split(key, N_LEAF)
    return lax.map(lambda leaf_key: symmetric_block(leaf_key, UPD).astype(jnp.bfloat16), leaf_keys)


def draw_top_coupling(key, part):
    key_block, key_below = jax.random.split(key, 2)
    win_cols = PW * N_BLK
    leading = symmetric_block(key_block, win_cols)
    below = jax.random.uniform(key_below, (TOP - win_cols, win_cols), jnp.float32, -0.5, 0.5)
    return jnp.concatenate([leading, below], axis=0).astype(jnp.bfloat16)


def levels(rng, extent, cuts, low, largest):
    loudness, own = 1.0, jax.random.fold_in(rng, 6)
    for dim, shards_of in cuts:
        steps = jnp.exp(jax.random.uniform(jax.random.fold_in(own, dim), (shards_of,), jnp.float32, low / len(cuts), largest / len(cuts)))
        loudness = loudness * jnp.repeat(steps, extent[dim] // shards_of).reshape([-1 if axis == dim else 1 for axis in range(len(extent))])
    return loudness


def bell_draw(own_key, extent, spread, bound, cuts=(), held_as=jnp.bfloat16):
    level = levels(own_key, extent, cuts, -0.22, 0.18) if cuts else 1.0
    values = jax.random.normal(own_key, extent, jnp.float32) * spread * level
    return jnp.minimum(jnp.maximum(values, -bound), bound).astype(held_as)


def setup_inputs(seed: int = 0) -> dict:
    key_of = jax.random.split(jax.random.key(seed), 7)
    leaf_net = bell_draw(key_of[0], (N_LEAF, NETS, UPD), (NETS // 4) ** -0.5, 1.5, ((0, 8),))
    leaf_coupling = draw_leaf_coupling(jax.random.fold_in(key_of[6], 71), 0)
    index_maps = draw_index_maps(jax.random.fold_in(key_of[6], 71), 0)
    sep_anchor = jnp.clip(jnp.exp(jax.random.uniform(key_of[3], (PARENTS, SEP), jnp.float32, math.log(0.5), math.log(4.0))), 0.5, 4.0)
    top_net = bell_draw(key_of[4], (NETS, TOP), (NETS // 4) ** -0.5, 1.5, ((1, 8),))
    top_coupling = draw_top_coupling(jax.random.fold_in(key_of[6], 71), 0)
    return dict(leaf_net=leaf_net, leaf_coupling=leaf_coupling, index_maps=index_maps, sep_anchor=sep_anchor, top_net=top_net, top_coupling=top_coupling)


def leaf_update(net_cols, coupling):
    gram_rows = jnp.dot(net_cols.T.astype(jnp.float32), net_cols.astype(jnp.float32), preferred_element_type=jnp.float32)
    return gram_rows + coupling.astype(jnp.float32)

def extend_add(front, update, block_map):
    positions = (block_map[:, None] * BS + jnp.arange(BS, dtype=jnp.int32)[None, :]).reshape(-1)
    return front.at[positions[:, None], positions[None, :]].add(update.astype(jnp.float32))

def eliminate(left_child, right_child, map_left, map_right, anchor_row):
    front_order = SEP + UPD
    front = jnp.zeros((front_order, front_order), jnp.float32)
    front = extend_add(front, left_child, map_left)
    front = extend_add(front, right_child, map_right)
    pivot_block = front[:SEP, :SEP] + jnp.diag(anchor_row)
    factor = jnp.linalg.cholesky(pivot_block)
    below_rows = jax.scipy.linalg.solve_triangular(factor, front[SEP:, :SEP].T, lower=True).T
    below_rows = below_rows.astype(jnp.bfloat16)
    schur_part = front[SEP:, SEP:] - jnp.dot(below_rows.astype(jnp.float32), below_rows.T.astype(jnp.float32), preferred_element_type=jnp.float32)
    return schur_part

def reference(leaf_net, leaf_coupling, index_maps, sep_anchor, top_net, top_coupling):
    updates = [leaf_update(leaf_net[leaf_num], leaf_coupling[leaf_num]) for leaf_num in range(N_LEAF)]
    node_base = 0
    parent_base = 0
    for level_num in range(LEVELS):
        parent_count = len(updates) // 2
        merged = []
        for parent_num in range(parent_count):
            merged.append(eliminate(updates[2 * parent_num], updates[2 * parent_num + 1], index_maps[node_base + 2 * parent_num], index_maps[node_base + 2 * parent_num + 1], sep_anchor[parent_base + parent_num]))
        node_base = node_base + len(updates)
        parent_base = parent_base + parent_count
        updates = merged
    root_list = jnp.stack(updates)
    root_update = jnp.repeat(root_list, 2 ** LEVELS, axis=0)
    win_cols = PW * N_BLK
    window = jnp.dot(top_net.T.astype(jnp.float32), top_net[:, :win_cols].astype(jnp.float32), preferred_element_type=jnp.float32)
    window = window + top_coupling.astype(jnp.float32)
    for panel_num in range(NF):
        panel_lo = panel_num * PW
        panel_hi = panel_lo + PW
        factor = jnp.linalg.cholesky(window[panel_lo:panel_hi, panel_lo:panel_hi])
        below_rows = jax.scipy.linalg.solve_triangular(factor, window[panel_hi:, panel_lo:panel_hi].T, lower=True).T
        panel_full = jnp.concatenate([jnp.zeros((panel_lo, PW), jnp.float32), factor, below_rows], axis=0)
        rounded = panel_full.astype(jnp.bfloat16)
        trailing = window[:, panel_hi:] - jnp.dot(rounded.astype(jnp.float32), rounded[panel_hi:win_cols].T.astype(jnp.float32), preferred_element_type=jnp.float32)
        window = jnp.concatenate([window[:, :panel_lo], panel_full, trailing], axis=1)
    return (root_update, window)
```

```python
import jax
import jax.numpy as jnp
from jax import lax
from jax.experimental import pallas as pl
from jax.experimental.pallas import tpu as pltpu
from jax.sharding import PartitionSpec as P

BS = 128
LEVELS = 2
PW = 512
GROUP = 2
LAST = (((1,), (1,)), ((), ()))
FIRST = (((0,), (0,)), ((), ()))
HIGH = lax.Precision.HIGHEST


def gram(left, right):
    return lax.dot_general(left, right, FIRST, preferred_element_type=jnp.float32)


def outer(left, right):
    return lax.dot_general(left, right, LAST, preferred_element_type=jnp.float32)


def solved(rows, inverse):
    return lax.dot_general(rows, inverse, LAST, precision=HIGH, preferred_element_type=jnp.float32)


def factor_inverse(block):
    factor = jnp.linalg.cholesky(block)
    identity = jnp.eye(block.shape[0], dtype=jnp.float32)
    return factor, jax.scipy.linalg.solve_triangular(factor, identity, lower=True)


def swapped(value, axis, mask):
    return lax.ppermute(value, axis, [(s, s ^ mask) for s in range(lax.axis_size(axis))])


def total(value, axis):
    mask = 1
    while mask < lax.axis_size(axis):
        value = value + swapped(value, axis, mask)
        mask *= 2
    return value


def leaf_spread(value, source_of):
    leaf_count, blk_count = lax.axis_size("leaf"), lax.axis_size("blk")
    blk_pos = lax.axis_index("blk")
    sources = jnp.array([source_of(b) for b in range(blk_count)], jnp.int32)
    rank = lax.axis_index("leaf") ^ sources[blk_pos]
    step = leaf_count // 2
    while step:
        pairs = []
        for b in range(blk_count):
            for r in range(0, leaf_count, 2 * step):
                src = source_of(b)
                pairs.append(((r ^ src) * blk_count + b, ((r + step) ^ src) * blk_count + b))
        got = lax.ppermute(value, ("leaf", "blk"), pairs)
        value = jnp.where(rank % (2 * step) == step, got, value)
        step //= 2
    return value


def first_two(value):
    blk_count = lax.axis_size("blk")
    blk_pos = lax.axis_index("blk")
    step = 2
    while step < blk_count:
        got = lax.ppermute(value, "blk", [(s, s + step) for s in range(step)])
        value = jnp.where((blk_pos >= step) & (blk_pos < 2 * step), got, value)
        step *= 2
    mate = swapped(value, "blk", 1)
    even = blk_pos % 2 == 0
    return jnp.where(even, value, mate), jnp.where(even, mate, value)


def merge_kernel(scal, own, oth, lrow, lall, out):
    blocks = own.shape[1] // BS
    first = scal[1] + GROUP * (scal[0] + pl.program_id(0))
    step = 4
    for quarter in range(blocks // step):
        width = step * BS
        prod = outer(lrow[...], lall[quarter * width : (quarter + 1) * width, :])
        for half in range(GROUP):
            row_a = scal[2 + first + half]
            row_b = scal[2 + blocks + first + half]
            at_a = pl.multiple_of((jnp.maximum(row_a, 0) % GROUP) * BS, BS)
            at_b = pl.multiple_of((jnp.maximum(row_b, 0) % GROUP) * BS, BS)
            for c in range(step):
                col = quarter * step + c
                col_a = scal[2 + col]
                col_b = scal[2 + blocks + col]
                ca = pl.multiple_of(jnp.maximum(col_a, 0) * BS, BS)
                cb = pl.multiple_of(jnp.maximum(col_b, 0) * BS, BS)
                a = own[pl.ds(at_a, BS), pl.ds(ca, BS)]
                b = oth[pl.ds(at_b, BS), pl.ds(cb, BS)]
                a = jnp.where((row_a >= 0) & (col_a >= 0), a, 0.0)
                b = jnp.where((row_b >= 0) & (col_b >= 0), b, 0.0)
                piece = prod[half * BS : (half + 1) * BS, c * BS : (c + 1) * BS]
                out[half * BS : (half + 1) * BS, col * BS : (col + 1) * BS] = a + b - piece


def merge(group_first, block_first, src_own, src_oth, own, oth, lrow, lall):
    rows, cols = oth.shape
    sep = lrow.shape[1]
    tall = GROUP * BS
    scal = jnp.concatenate(
        [jnp.stack([jnp.int32(group_first), jnp.int32(block_first)]), src_own, src_oth]
    )
    spec = pltpu.PrefetchScalarGridSpec(
        num_scalar_prefetch=1,
        grid=(rows // tall,),
        in_specs=[
            pl.BlockSpec((tall, cols), lambda i, s: (s[0] + i, 0)),
            pl.BlockSpec((tall, cols), lambda i, s: (i, 0)),
            pl.BlockSpec((tall, sep), lambda i, s: (s[0] + i, 0)),
            pl.BlockSpec((cols, sep), lambda i, s: (0, 0)),
        ],
        out_specs=pl.BlockSpec((tall, cols), lambda i, s: (s[0] + i, 0)),
    )
    return pl.pallas_call(
        merge_kernel,
        out_shape=jax.ShapeDtypeStruct(own.shape, jnp.float32),
        grid_spec=spec,
        input_output_aliases={1: 0},
        compiler_params=pltpu.CompilerParams(vmem_limit_bytes=48 * 2**20),
        cost_estimate=pl.CostEstimate(
            flops=2 * rows * cols * sep,
            bytes_accessed=12 * rows * cols + 2 * sep * cols,
            transcendentals=0,
        ),
    )(scal, own, oth, lrow, lall)


def sources(block_map, first, count):
    targets = first + jnp.arange(count, dtype=jnp.int32)
    match = targets[:, None] == block_map[None, :]
    ids = jnp.arange(block_map.shape[0], dtype=jnp.int32)[None, :]
    return jnp.max(jnp.where(match, ids, -1), axis=1)


def take_columns(rows, src):
    return jnp.concatenate(
        [lax.dynamic_slice_in_dim(rows, src[k] * BS, BS, 1) for k in range(src.shape[0])], axis=1
    )


def take_rows(rows, picks, keeps):
    parts = [
        jnp.where(keeps[k], lax.dynamic_slice_in_dim(rows, picks[k] * BS, BS, 0), 0.0)
        for k in range(picks.shape[0])
    ]
    return jnp.concatenate(parts, axis=0)


def front_columns(cols, upd_src, sep_src, block_first, block_rows):
    local = lax.dynamic_slice_in_dim(upd_src, block_first, block_rows, 0)
    below = take_rows(cols, jnp.maximum(local - block_first, 0), local >= 0)
    here = (sep_src >= block_first) & (sep_src < block_first + block_rows)
    pivot = take_rows(cols, jnp.where(here, sep_src - block_first, 0), here)
    return below, pivot


def top_part(top_net, top_coupling):
    leaf_pos, blk_pos = lax.axis_index("leaf"), lax.axis_index("blk")
    rows_top = top_net.shape[1]
    lead = 2 * PW
    coup0, coup1 = first_two(top_coupling)
    piece = lax.dynamic_slice_in_dim(top_net, (blk_pos * PW) % rows_top, PW, 1)
    net_mine = leaf_spread(piece, lambda b: (b * PW) // rows_top)
    lead_mine = leaf_spread(top_coupling[:lead], lambda b: 0)
    both0, both1 = first_two(jnp.concatenate([lead_mine, net_mine], axis=0))
    lead0, net0 = both0[:lead].astype(jnp.float32), both0[lead:]
    lead1, net1 = both1[:lead].astype(jnp.float32), both1[lead:]
    mine = lead_mine.astype(jnp.float32)
    factor0, inv0 = factor_inverse(gram(net0, net0) + lead0[:PW])
    cross = solved(gram(net1, net0) + lead0[PW:], inv0).astype(jnp.bfloat16)
    factor1, inv1 = factor_inverse(gram(net1, net1) + lead1[PW:] - outer(cross, cross))
    q0 = solved((gram(net0, net_mine) + mine[:PW]).T, inv0).astype(jnp.bfloat16)
    q1 = solved((gram(net1, net_mine) + mine[PW:]).T - outer(q0, cross), inv1)
    q1 = q1.astype(jnp.bfloat16)
    holds = leaf_pos == 0
    row = (leaf_pos * rows_top + jnp.arange(rows_top, dtype=jnp.int32))[:, None]

    def panel(current, inverse, factor, first):
        full = solved(current, inverse)
        placed = lax.dynamic_update_slice(full, factor, (first, 0))
        full = jnp.where(holds, placed, full)
        return jnp.where(row >= first, full, 0.0)

    p0 = panel(gram(top_net, net0) + coup0.astype(jnp.float32), inv0, factor0, 0)
    b0 = p0.astype(jnp.bfloat16)
    p1 = panel(
        gram(top_net, net1) + coup1.astype(jnp.float32) - outer(b0, cross), inv1, factor1, PW
    )
    b1 = p1.astype(jnp.bfloat16)
    rest = gram(top_net, net_mine) + top_coupling.astype(jnp.float32)
    rest = rest - outer(b0, q0) - outer(b1, q1)
    return jnp.where(blk_pos == 0, p0, jnp.where(blk_pos == 1, p1, rest))


def per_device(leaf_net, leaf_coupling, index_maps, sep_anchor, top_net, top_coupling):
    leaf_count = lax.axis_size("leaf")
    leaf_pos, blk_pos = lax.axis_index("leaf"), lax.axis_index("blk")
    net_own = leaf_net[0]
    coup_own = leaf_coupling[0]
    rows_dev, upd_order = coup_own.shape
    sep_order = sep_anchor.shape[1]
    block_rows = rows_dev // BS
    sep_blocks, upd_blocks = sep_order // BS, upd_order // BS
    block_first = blk_pos * block_rows
    groups = block_rows // GROUP

    def my_part(net):
        return lax.dynamic_slice_in_dim(net, blk_pos * rows_dev, rows_dev, 1)

    def maps(base, node):
        row = lax.dynamic_index_in_dim(index_maps, base + node, 0, keepdims=False)
        return sources(row, 0, sep_blocks), sources(row, sep_blocks, upd_blocks)

    def factor_columns(cols_own, cols_oth, own, oth, anchor):
        below_a, pivot_a = front_columns(cols_own, own[1], own[0], block_first, block_rows)
        below_b, pivot_b = front_columns(cols_oth, oth[1], oth[0], block_first, block_rows)
        pivot = total(pivot_a + pivot_b, "blk") + jnp.diag(anchor)
        inverse = factor_inverse(pivot)[1]
        lrow = solved(below_a + below_b, inverse).astype(jnp.bfloat16)
        return lrow, lax.all_gather(lrow, "blk", axis=0, tiled=True)

    own, oth = maps(0, leaf_pos), maps(0, leaf_pos ^ 1)
    net_oth = swapped(net_own, "leaf", 1)
    coup_cols = take_columns(coup_own, own[0])
    coup_cols_oth = swapped(coup_cols, "leaf", 1)
    coup_oth = swapped(coup_own, "leaf", 1)
    cols_own = gram(my_part(net_own), take_columns(net_own, own[0])) + coup_cols.astype(jnp.float32)
    cols_oth = gram(my_part(net_oth), take_columns(net_oth, oth[0])) + coup_cols_oth.astype(
        jnp.float32
    )
    lrow, lall = factor_columns(cols_own, cols_oth, own, oth, sep_anchor[leaf_pos >> 1])
    u_own = gram(my_part(net_own), net_own) + coup_own.astype(jnp.float32)
    u_oth = gram(my_part(net_oth), net_oth) + coup_oth.astype(jnp.float32)
    update = merge(0, block_first, own[1], oth[1], u_own, u_oth, lrow, lall)

    node = leaf_pos >> 1
    own, oth = maps(leaf_count, node), maps(leaf_count, node ^ 1)
    cols_own = take_columns(update, own[0])
    cols_oth = swapped(cols_own, "leaf", 2)
    tall = GROUP * BS
    pieces = []
    if groups % 2 == 0:
        side = leaf_pos & 1
        half = groups // 2
        direct = []
        for k in range(half):
            at = side * half + k
            piece = lax.dynamic_slice_in_dim(update, at * tall, tall, 0)
            direct.append((at, swapped(piece, "leaf", 2)))
        pieces = direct + [
            ((1 - side) * half + k, swapped(direct[k][1], "leaf", 1)) for k in range(half)
        ]
    else:
        pieces = [(0, swapped(update, "leaf", 2))]
    anchor = sep_anchor[leaf_count // 2 + (node >> 1)]
    lrow, lall = factor_columns(cols_own, cols_oth, own, oth, anchor)
    window = top_part(top_net, top_coupling)
    for at, piece in pieces:
        update = merge(at, block_first, own[1], oth[1], update, piece, lrow, lall)
    return (update[None], window)


def solution(mesh):
    return jax.shard_map(
        per_device,
        mesh=mesh,
        in_specs=(
            P("leaf", None, None),
            P("leaf", "blk", None),
            P(),
            P(),
            P(None, "leaf"),
            P("leaf", "blk"),
        ),
        out_specs=(P("leaf", "blk", None), P("leaf", "blk")),
        check_vma=False,
    )
```

```python
import jax
import jax.numpy as jnp
from jax import lax
from jax.experimental import pallas as pl
from jax.experimental.pallas import tpu as pltpu
from jax.sharding import PartitionSpec as P

BS = 128
LEVELS = 2
PW = 512
GROUP = 2
LAST = (((1,), (1,)), ((), ()))
FIRST = (((0,), (0,)), ((), ()))
HIGH = lax.Precision.HIGHEST


def gram(left, right):
    return lax.dot_general(left, right, FIRST, preferred_element_type=jnp.float32)


def outer(left, right):
    return lax.dot_general(left, right, LAST, preferred_element_type=jnp.float32)


def solved(rows, inverse):
    return jnp.dot(rows, inverse, precision=HIGH, preferred_element_type=jnp.float32)


def inverse_factor(block):
    order = block.shape[0]
    small = jnp.eye(BS, dtype=jnp.float32)
    rest = jnp.concatenate([block, jnp.eye(order, dtype=jnp.float32)], axis=0)
    columns = []
    for at in range(0, order, BS):
        factor = jnp.linalg.cholesky(rest[at : at + BS, :BS])
        inverse = jax.scipy.linalg.solve_triangular(factor, small, lower=True)
        column = solved(rest[:, :BS], inverse.T)
        columns.append(column[order:])
        if at + BS < order:
            rest = rest[:, BS:] - solved(column, column[at + BS : order].T)
    return jnp.concatenate(columns, axis=1)


def inverse_pair(tree_block, top_block):
    low = (lax.axis_index("blk") // 2) % 2 == 0
    mine = inverse_factor(jnp.where(low, tree_block, top_block))
    mate = swapped(mine, "blk", 2)
    return jnp.where(low, mine, mate), jnp.where(low, mate, mine)


def swapped(value, axis, mask):
    return lax.ppermute(value, axis, [(s, s ^ mask) for s in range(lax.axis_size(axis))])


def total(value, axis):
    mask = 1
    while mask < lax.axis_size(axis):
        value = value + swapped(value, axis, mask)
        mask *= 2
    return value


def leaf_spread(value, source_of):
    leaf_count, blk_count = lax.axis_size("leaf"), lax.axis_size("blk")
    blk_pos = lax.axis_index("blk")
    sources = jnp.array([source_of(b) for b in range(blk_count)], jnp.int32)
    rank = lax.axis_index("leaf") ^ sources[blk_pos]
    step = leaf_count // 2
    while step:
        pairs = []
        for b in range(blk_count):
            for r in range(0, leaf_count, 2 * step):
                src = source_of(b)
                pairs.append(((r ^ src) * blk_count + b, ((r + step) ^ src) * blk_count + b))
        got = lax.ppermute(value, ("leaf", "blk"), pairs)
        value = jnp.where(rank % (2 * step) == step, got, value)
        step //= 2
    return value


def first_two(value):
    blk_count = lax.axis_size("blk")
    blk_pos = lax.axis_index("blk")
    step = 2
    while step < blk_count:
        got = lax.ppermute(value, "blk", [(s, s + step) for s in range(step)])
        value = jnp.where((blk_pos >= step) & (blk_pos < 2 * step), got, value)
        step *= 2
    mate = swapped(value, "blk", 1)
    even = blk_pos % 2 == 0
    return jnp.where(even, value, mate), jnp.where(even, mate, value)


def merge_kernel(scal, own, oth, lrow, lall, out):
    blocks = own.shape[1] // BS
    first = scal[1] + GROUP * (scal[0] + pl.program_id(0))
    step = 4
    for quarter in range(blocks // step):
        width = step * BS
        prod = outer(lrow[...], lall[quarter * width : (quarter + 1) * width, :])
        for half in range(GROUP):
            row_a = scal[2 + first + half]
            row_b = scal[2 + blocks + first + half]
            at_a = pl.multiple_of((jnp.maximum(row_a, 0) % GROUP) * BS, BS)
            at_b = pl.multiple_of((jnp.maximum(row_b, 0) % GROUP) * BS, BS)
            for c in range(step):
                col = quarter * step + c
                col_a = scal[2 + col]
                col_b = scal[2 + blocks + col]
                ca = pl.multiple_of(jnp.maximum(col_a, 0) * BS, BS)
                cb = pl.multiple_of(jnp.maximum(col_b, 0) * BS, BS)
                a = own[pl.ds(at_a, BS), pl.ds(ca, BS)]
                b = oth[pl.ds(at_b, BS), pl.ds(cb, BS)]
                a = jnp.where((row_a >= 0) & (col_a >= 0), a, 0.0)
                b = jnp.where((row_b >= 0) & (col_b >= 0), b, 0.0)
                piece = prod[half * BS : (half + 1) * BS, c * BS : (c + 1) * BS]
                out[half * BS : (half + 1) * BS, col * BS : (col + 1) * BS] = a + b - piece


def merge(group_first, block_first, src_own, src_oth, own, oth, lrow, lall):
    rows, cols = oth.shape
    sep = lrow.shape[1]
    tall = GROUP * BS
    scal = jnp.concatenate(
        [jnp.stack([jnp.int32(group_first), jnp.int32(block_first)]), src_own, src_oth]
    )
    spec = pltpu.PrefetchScalarGridSpec(
        num_scalar_prefetch=1,
        grid=(rows // tall,),
        in_specs=[
            pl.BlockSpec((tall, cols), lambda i, s: (s[0] + i, 0)),
            pl.BlockSpec((tall, cols), lambda i, s: (i, 0)),
            pl.BlockSpec((tall, sep), lambda i, s: (s[0] + i, 0)),
            pl.BlockSpec((cols, sep), lambda i, s: (0, 0)),
        ],
        out_specs=pl.BlockSpec((tall, cols), lambda i, s: (s[0] + i, 0)),
    )
    return pl.pallas_call(
        merge_kernel,
        out_shape=jax.ShapeDtypeStruct(own.shape, jnp.float32),
        grid_spec=spec,
        input_output_aliases={1: 0},
        compiler_params=pltpu.CompilerParams(vmem_limit_bytes=48 * 2**20),
        cost_estimate=pl.CostEstimate(
            flops=2 * rows * cols * sep,
            bytes_accessed=12 * rows * cols + 2 * sep * cols,
            transcendentals=0,
        ),
    )(scal, own, oth, lrow, lall)


def sources(block_map, first, count):
    targets = first + jnp.arange(count, dtype=jnp.int32)
    match = targets[:, None] == block_map[None, :]
    ids = jnp.arange(block_map.shape[0], dtype=jnp.int32)[None, :]
    return jnp.max(jnp.where(match, ids, -1), axis=1)


def take_columns(rows, src):
    return jnp.concatenate(
        [lax.dynamic_slice_in_dim(rows, src[k] * BS, BS, 1) for k in range(src.shape[0])], axis=1
    )


def take_rows(rows, picks, keeps):
    parts = [
        jnp.where(keeps[k], lax.dynamic_slice_in_dim(rows, picks[k] * BS, BS, 0), 0.0)
        for k in range(picks.shape[0])
    ]
    return jnp.concatenate(parts, axis=0)


def front_columns(cols, upd_src, sep_src, block_first, block_rows):
    local = lax.dynamic_slice_in_dim(upd_src, block_first, block_rows, 0)
    below = take_rows(cols, jnp.maximum(local - block_first, 0), local >= 0)
    here = (sep_src >= block_first) & (sep_src < block_first + block_rows)
    pivot = take_rows(cols, jnp.where(here, sep_src - block_first, 0), here)
    return below, pivot


def per_device(leaf_net, leaf_coupling, index_maps, sep_anchor, top_net, top_coupling):
    leaf_count = lax.axis_size("leaf")
    leaf_pos, blk_pos = lax.axis_index("leaf"), lax.axis_index("blk")
    net_own = leaf_net[0]
    coup_own = leaf_coupling[0]
    rows_dev, upd_order = coup_own.shape
    sep_order = sep_anchor.shape[1]
    block_rows = rows_dev // BS
    sep_blocks, upd_blocks = sep_order // BS, upd_order // BS
    block_first = blk_pos * block_rows
    groups = block_rows // GROUP

    def my_part(net):
        return lax.dynamic_slice_in_dim(net, blk_pos * rows_dev, rows_dev, 1)

    def maps(base, node):
        row = lax.dynamic_index_in_dim(index_maps, base + node, 0, keepdims=False)
        return sources(row, 0, sep_blocks), sources(row, sep_blocks, upd_blocks)

    def columns_and_pivot(cols_own, cols_oth, own, oth, anchor):
        below_a, pivot_a = front_columns(cols_own, own[1], own[0], block_first, block_rows)
        below_b, pivot_b = front_columns(cols_oth, oth[1], oth[0], block_first, block_rows)
        return below_a + below_b, total(pivot_a + pivot_b, "blk") + jnp.diag(anchor)

    def eliminated(below, inverse):
        lrow = solved(below, inverse).astype(jnp.bfloat16)
        return lrow, lax.all_gather(lrow, "blk", axis=0, tiled=True)

    rows_top = top_net.shape[1]
    lead = 2 * PW
    row = (leaf_pos * rows_top + jnp.arange(rows_top, dtype=jnp.int32))[:, None]
    col = jnp.arange(PW, dtype=jnp.int32)[None, :]

    def panel(current, inverse, first):
        return jnp.where(row - first >= col, solved(current, inverse), 0.0)

    own, oth = maps(0, leaf_pos), maps(0, leaf_pos ^ 1)
    net_oth = swapped(net_own, "leaf", 1)
    coup_cols = take_columns(coup_own, own[0])
    coup_cols_oth = swapped(coup_cols, "leaf", 1)
    piece = lax.dynamic_slice_in_dim(top_net, (blk_pos * PW) % rows_top, PW, 1)
    net_mine = leaf_spread(piece, lambda b: (b * PW) // rows_top)
    lead_mine = leaf_spread(top_coupling[:lead], lambda b: 0)
    net_oth, coup_cols_oth, lead_mine, net_mine, coup_own = lax.optimization_barrier(
        (net_oth, coup_cols_oth, lead_mine, net_mine, coup_own)
    )
    coup_oth = swapped(coup_own, "leaf", 1)
    both0, both1 = first_two(jnp.concatenate([lead_mine, net_mine], axis=0))
    both0, both1, top_late = lax.optimization_barrier((both0, both1, top_coupling))
    coup0, coup1 = first_two(top_late)
    lead0, net0 = both0[:lead].astype(jnp.float32), both0[lead:]
    lead1, net1 = both1[:lead].astype(jnp.float32), both1[lead:]
    mine = lead_mine.astype(jnp.float32)
    cols_own = gram(my_part(net_own), take_columns(net_own, own[0])) + coup_cols.astype(jnp.float32)
    cols_oth = gram(my_part(net_oth), take_columns(net_oth, oth[0])) + coup_cols_oth.astype(
        jnp.float32
    )
    below, pivot = columns_and_pivot(cols_own, cols_oth, own, oth, sep_anchor[leaf_pos >> 1])
    inverse, inv0 = inverse_pair(pivot, gram(net0, net0) + lead0[:PW])
    lrow, lall = eliminated(below, inverse)
    u_own = gram(my_part(net_own), net_own) + coup_own.astype(jnp.float32)
    u_oth = gram(my_part(net_oth), net_oth) + coup_oth.astype(jnp.float32)
    update = merge(0, block_first, own[1], oth[1], u_own, u_oth, lrow, lall)

    node = leaf_pos >> 1
    own, oth = maps(leaf_count, node), maps(leaf_count, node ^ 1)
    cols_own = take_columns(update, own[0])
    cols_oth = swapped(cols_own, "leaf", 2)
    tall = GROUP * BS
    pieces = []
    if groups % 2 == 0:
        side = leaf_pos & 1
        half = groups // 2
        direct = []
        for k in range(half):
            at = side * half + k
            piece = lax.dynamic_slice_in_dim(update, at * tall, tall, 0)
            direct.append((at, swapped(piece, "leaf", 2)))
        pieces = direct + [
            ((1 - side) * half + k, swapped(direct[k][1], "leaf", 1)) for k in range(half)
        ]
    else:
        pieces = [(0, swapped(update, "leaf", 2))]
    anchor = sep_anchor[leaf_count // 2 + (node >> 1)]
    below, pivot = columns_and_pivot(cols_own, cols_oth, own, oth, anchor)
    cross = solved(gram(net1, net0) + lead0[PW:], inv0).astype(jnp.bfloat16)
    inverse, inv1 = inverse_pair(
        pivot, gram(net1, net1) + lead1[PW:] - outer(cross, cross)
    )
    lrow, lall = eliminated(below, inverse)
    q0 = solved((gram(net0, net_mine) + mine[:PW]).T, inv0).astype(jnp.bfloat16)
    q1 = solved((gram(net1, net_mine) + mine[PW:]).T - outer(q0, cross), inv1)
    q1 = q1.astype(jnp.bfloat16)
    p0 = panel(gram(top_net, net0) + coup0.astype(jnp.float32), inv0, 0)
    b0 = p0.astype(jnp.bfloat16)
    x1 = gram(top_net, net1) + coup1.astype(jnp.float32) - outer(b0, cross)
    p1 = panel(x1, inv1, PW)
    rest = gram(top_net, net_mine) + top_coupling.astype(jnp.float32) - outer(b0, q0)
    rest = rest - outer(p1.astype(jnp.bfloat16), q1)
    window = jnp.where(blk_pos == 0, p0, jnp.where(blk_pos == 1, p1, rest))
    for at, piece in pieces:
        update = merge(at, block_first, own[1], oth[1], update, piece, lrow, lall)
    return (update[None], window)


def solution(mesh):
    return jax.shard_map(
        per_device,
        mesh=mesh,
        in_specs=(
            P("leaf", None, None),
            P("leaf", "blk", None),
            P(),
            P(),
            P(None, "leaf"),
            P("leaf", "blk"),
        ),
        out_specs=(P("leaf", "blk", None), P("leaf", "blk")),
        check_vma=False,
    )
```
